32 devices in a mesh: ctx: 8 (over z, x), col: 4 (over y, core).
Axes of the slice: x: 2, y: 2, z: 4, core: 2. Of those that a mesh axis runs over, the one named last changes fastest.
Arguments:
- sequence: bfloat16 [4096, 4096], P('ctx', 'col'), may hold values from -6 to 6
- w_proj: bfloat16 [4096, 3, 2048], P('col'), may hold values from -0.125 to 0.125
- short_filter: float32 [3, 3, 2048], P(None, None, 'col'), may hold values from -3 to 3
- long_filter: float32 [4096, 2048], P('ctx', 'col'), may hold values from -0.09375 to 0.09375
- skip_gain: float32 [2048], P('col'), may hold values from 0.5 to 1.5
Outputs:
- mixed: float32 [4096, 2048], P('ctx', 'col')
The draws below stay inside these ranges and needn't reach their ends.
All inputs are finite; a program needn't handle non-finite values.
Results may differ from the reference program's by a relative error of at most 0.0003.
Values sent between devices are 32-bit elements; how exact they have to be, the bound alone decides.
No kernel may reach another device: no remote copies, remote signals or barrier semaphores. Data moves between devices by JAX's collectives and lax.ppermute only.
A program may use at most 128 MiB of HBM per device.

```python
import jax
import jax.numpy as jnp
from jax import lax

D = 4096
C = 2048
TOK_DEV = 512
TOKENS = 4096


def strengthened(drawn, own_key, source, target, shards_of, factor):
    def block_of(axis_at):
        return (jnp.arange(drawn.shape[axis_at]) // (drawn.shape[axis_at] // shards_of)).reshape((-1,) + (1,) * (drawn.ndim - 1 - axis_at))

    one_side = jax.random.permutation(own_key, shards_of)[block_of(target)]
    second = (block_of(target) + shards_of // 2) % shards_of
    return jnp.where((block_of(source) == one_side) | (block_of(source) == second), factor * drawn, drawn)


def steps_of(own_key, dims, pieces, low, largest):
    level = 1.0
    for axis_at, parts in pieces:
        steps = jax.random.uniform(jax.random.fold_in(jax.random.fold_in(own_key, 6), axis_at), (parts,), jnp.float32, low / len(pieces), largest / len(pieces))
        level = level * jnp.repeat(jnp.exp(steps), dims[axis_at] // parts).reshape((-1,) + (1,) * (len(dims) - 1 - axis_at))
    return level


def centred(own_key, dims, spread, reach, cuts=(), dtype=jnp.bfloat16):
    level = steps_of(own_key, dims, cuts, -0.22, 0.18) if cuts else 1.0
    result = jax.random.normal(own_key, dims, jnp.float32) * spread * level
    return jnp.minimum(jnp.maximum(result, -reach), reach).astype(dtype)


def heavy_noise(stream_key, dims, spread, most, pieces, heavy, held_as=jnp.bfloat16):
    result = spread * jax.random.normal(stream_key, dims, jnp.float32)
    if pieces:
        result = result * steps_of(stream_key, dims, pieces, -0.22, 0.18)
    return jnp.clip(strengthened(result, jax.random.fold_in(stream_key, 3), *heavy), -most, most).astype(held_as)


def setup_inputs(seed: int = 0) -> dict:
    keys = jax.random.split(jax.random.key(seed), 6)
    sequence = centred(keys[0], (TOKENS, D), 1.0, 6.0, ((0, 8), (1, 4)))
    w_proj = heavy_noise(keys[1], (D, 3, C), D ** -0.5, 0.125, ((0, 4),), (0, 2, 4, 2.0))
    short_filter = centred(keys[2], (3, 3, C), 0.6, 3.0, ((2, 4),), jnp.float32)
    long_filter = centred(keys[3], (TOKENS, C), TOKENS ** -0.5, 0.09375, ((0, 8), (1, 4)), jnp.float32)
    skip_gain = jnp.clip(0.5 + 1.0 * jax.random.uniform(keys[4], (C,), jnp.float32) ** steps_of(keys[4], (C,), ((0, 4),), -0.2, 0.2), 0.5, 1.5)
    return {"sequence": sequence, "w_proj": w_proj, "short_filter": short_filter, "long_filter": long_filter, "skip_gain": skip_gain}


def reference(sequence, w_proj, short_filter, long_filter, skip_gain):
    flat_weight = w_proj.reshape(D, 3 * C)
    blocks = sequence.reshape(TOKENS // TOK_DEV, TOK_DEV, D)

    def project(block):
        return jnp.dot(block, flat_weight, preferred_element_type=jnp.float32)

    projected = lax.map(project, blocks).reshape(TOKENS, 3, C)
    shaped = short_filter[0] * projected + short_filter[1] * jnp.roll(projected, 1, axis=0) + short_filter[2] * jnp.roll(projected, 2, axis=0)
    query_rows = shaped[:, 0, :]
    gated_values = shaped[:, 1, :] * shaped[:, 2, :]
    spectrum = jnp.fft.rfft(gated_values, axis=0) * jnp.fft.rfft(long_filter, axis=0)
    convolved = jnp.fft.irfft(spectrum, n=TOKENS, axis=0)
    return (query_rows * (convolved + skip_gain * gated_values)).astype(jnp.float32)
```

```python
import functools
import math

import jax
import jax.numpy as jnp
import numpy as np
from jax import lax
from jax.experimental import pallas as pl
from jax.experimental.pallas import tpu as pltpu
from jax.sharding import PartitionSpec as P

LANES = 128
SUBLANES = 8

VMEM_SPEC = pl.BlockSpec(memory_space=pltpu.VMEM)


def turned(pair, count, length):
    real, imag = pair
    c = math.cos(2.0 * math.pi * count / length)
    s = math.sin(2.0 * math.pi * count / length)
    return (real * c + imag * s, imag * c - real * s)


def real_forward(blocks):
    count = len(blocks)
    if count == 2:
        return [(blocks[0] + blocks[1], None), (blocks[0] - blocks[1], None)]
    half, quarter = count // 2, count // 4
    even, odd = real_forward(blocks[0::2]), real_forward(blocks[1::2])
    terms = [None] * (half + 1)
    for k in range(quarter + 1):
        even_real, even_imag = even[k]
        if k == 0:
            terms[0] = (even_real + odd[0][0], None)
            terms[half] = (even_real - odd[0][0], None)
        elif k == quarter:
            terms[k] = (even_real, -odd[k][0])
        else:
            odd_real, odd_imag = turned(odd[k], k, count)
            terms[k] = (even_real + odd_real, even_imag + odd_imag)
            terms[half - k] = (even_real - odd_real, odd_imag - even_imag)
    return terms


def real_inverse(terms):
    half = len(terms) - 1
    count = 2 * half
    if count == 2:
        return [terms[0][0] + terms[1][0], terms[0][0] - terms[1][0]]
    quarter = half // 2
    even, odd = [], []
    for k in range(quarter + 1):
        (a_real, a_imag), (b_real, b_imag) = terms[k], terms[half - k]
        if k == 0:
            even.append((a_real + b_real, None))
            odd.append((a_real - b_real, None))
        elif k == quarter:
            even.append((2.0 * a_real, None))
            odd.append((-2.0 * a_imag, None))
        else:
            even.append((a_real + b_real, a_imag - b_imag))
            odd.append(turned((a_real - b_real, a_imag + b_imag), -k, count))
    result = [None] * count
    result[0::2] = real_inverse(even)
    result[1::2] = real_inverse(odd)
    return result


def split_table(table):
    table = jnp.asarray(table, jnp.float32)
    high = table.astype(jnp.bfloat16)
    return jnp.stack([high, (table - high.astype(jnp.float32)).astype(jnp.bfloat16)])


def tables(blocks):
    step = np.arange(LANES)
    angle = 2.0 * np.pi / LANES * (step[:, None] * step[None, :] % LANES)
    c, s = np.cos(angle), np.sin(angle)
    forward = np.block([[c, -s], [s, c]])
    total = blocks * LANES
    turn = 2.0 * np.pi / total * (np.arange(blocks // 2 + 1)[:, None] * step[None, :])
    turns = np.stack([np.cos(turn), np.sin(turn)])[:, :, None, :]
    return (
        split_table(forward),
        split_table(forward.T),
        jnp.asarray(turns, jnp.float32),
    )


def split_dot(left, table_ref):
    high = left.astype(jnp.bfloat16)
    low = (left - high.astype(jnp.float32)).astype(jnp.bfloat16)
    dot = functools.partial(jnp.dot, preferred_element_type=jnp.float32)
    return dot(high, table_ref[0]) + (dot(low, table_ref[0]) + dot(high, table_ref[1]))


def lane_blocks(ref, rows):
    sources, _, width = ref.shape
    return [
        ref[p, rows, i * LANES : (i + 1) * LANES]
        for p in range(sources)
        for i in range(width // LANES)
    ]


def forward_rows(in_ref, stage_ref, turns_ref):
    channels = in_ref.shape[1]

    def group(g, carry):
        rows = pl.ds(pl.multiple_of(g * SUBLANES, SUBLANES), SUBLANES)
        for k, (real, imag) in enumerate(real_forward(lane_blocks(in_ref, rows))):
            c, s = turns_ref[0, k], turns_ref[1, k]
            if imag is None:
                stage_ref[k, rows, :LANES] = real * c
                stage_ref[k, rows, LANES:] = -(real * s)
            else:
                stage_ref[k, rows, :LANES] = real * c + imag * s
                stage_ref[k, rows, LANES:] = imag * c - real * s
        return carry

    lax.fori_loop(0, channels // SUBLANES, group, 0)


def spectrum_kernel(scale, in_ref, table_ref, turns_ref, out_ref, stage_ref):
    terms, channels, width = stage_ref.shape
    forward_rows(in_ref, stage_ref, turns_ref)
    rows = stage_ref[...].reshape(terms * channels, width)
    out_ref[...] = (split_dot(rows, table_ref) * scale).reshape(terms, channels, width)


def convolve_kernel(
    in_ref, spectrum_ref, forward_ref, inverse_ref, turns_ref, out_ref, stage_ref
):
    terms, channels, width = stage_ref.shape
    forward_rows(in_ref, stage_ref, turns_ref)
    rows = stage_ref[...].reshape(terms * channels, width)
    signal = split_dot(rows, forward_ref)
    other = spectrum_ref[...].reshape(terms * channels, width)
    s_real, s_imag = signal[:, :LANES], signal[:, LANES:]
    f_real, f_imag = other[:, :LANES], other[:, LANES:]
    product = jnp.concatenate(
        [s_real * f_real - s_imag * f_imag, s_real * f_imag + s_imag * f_real], axis=1
    )
    stage_ref[...] = split_dot(product, inverse_ref).reshape(terms, channels, width)
    sources, _, tokens = in_ref.shape
    per_source = tokens // LANES

    def group(g, carry):
        group_rows = pl.ds(pl.multiple_of(g * SUBLANES, SUBLANES), SUBLANES)
        pairs = []
        for k in range(terms):
            real = stage_ref[k, group_rows, :LANES]
            imag = stage_ref[k, group_rows, LANES:]
            c, s = turns_ref[0, k], turns_ref[1, k]
            pairs.append((real * c - imag * s, imag * c + real * s))
        for m, block in enumerate(real_inverse(pairs)):
            i = m % per_source
            out_ref[m // per_source, group_rows, i * LANES : (i + 1) * LANES] = block
        return carry

    lax.fori_loop(0, channels // SUBLANES, group, 0)


def stage_shape(shape):
    sources, channels, tokens = shape
    return (sources * tokens // LANES // 2 + 1, channels, 2 * LANES)


def spectrum(received, forward, turns):
    staged = stage_shape(received.shape)
    scale = 1.0 / (received.shape[0] * received.shape[2])
    return pl.pallas_call(
        functools.partial(spectrum_kernel, scale),
        out_shape=jax.ShapeDtypeStruct(staged, jnp.float32),
        in_specs=[VMEM_SPEC] * 3,
        out_specs=VMEM_SPEC,
        scratch_shapes=[pltpu.VMEM(staged, jnp.float32)],
        name="spectrum",
    )(received, forward, turns)


def convolve(received, filter_spectrum, first, forward, inverse, turns):
    staged = stage_shape(received.shape)
    block = first // staged[1]
    whole = lambda shape: pl.BlockSpec(shape, lambda i: (0,) * len(shape))
    return pl.pallas_call(
        convolve_kernel,
        grid=(1,),
        out_shape=jax.ShapeDtypeStruct(received.shape, jnp.float32),
        in_specs=[
            whole(received.shape),
            pl.BlockSpec(staged, lambda i: (0, block, 0)),
            whole(forward.shape),
            whole(inverse.shape),
            whole(turns.shape),
        ],
        out_specs=whole(received.shape),
        scratch_shapes=[pltpu.VMEM(staged, jnp.float32)],
        name="convolve",
    )(received, filter_spectrum, forward, inverse, turns)


def project_kernel(owner_ref, x_ref, w_ref, out_ref):
    del owner_ref
    rows = x_ref[...].astype(w_ref.dtype)
    out_ref[0] = jnp.dot(rows, w_ref[0], preferred_element_type=jnp.float32)


def project(rows, weight, owner, owner_width, start, width, first, count):
    tokens, depth = rows.shape
    per_owner, offset = owner_width // width, start // width
    return pl.pallas_call(
        project_kernel,
        grid_spec=pltpu.PrefetchScalarGridSpec(
            num_scalar_prefetch=1,
            grid=(count,),
            in_specs=[
                pl.BlockSpec((tokens, depth), lambda j, o: (0, 0)),
                pl.BlockSpec(
                    (1, depth, width), lambda j, o: (first + j, 0, o[0] * per_owner + offset)
                ),
            ],
            out_specs=pl.BlockSpec((1, tokens, width), lambda j, o: (j, 0, 0)),
        ),
        out_shape=jax.ShapeDtypeStruct((count, tokens, width), jnp.float32),
        name="project",
    )(owner, rows, weight)


def short_filtered(tap_ref, j, ext_ref, slot, tokens, start, size):
    lead = ext_ref.shape[1] - tokens
    taken = lambda back: ext_ref[slot, pl.ds(lead + start - back, size), :]
    return (
        tap_ref[0, j : j + 1, :] * taken(0)
        + tap_ref[1, j : j + 1, :] * taken(1)
        + tap_ref[2, j : j + 1, :] * taken(2)
    )


def fill_extended(ext_ref, slot, parts, rims, source):
    lead = rims[0].shape[1]
    rim = rims[0][source]
    for ref in rims[1:]:
        rim = rim + ref[source]
    body = parts[0][slot]
    for ref in parts[1:]:
        body = body + ref[slot]
    ext_ref[slot, :lead, :] = rim
    ext_ref[slot, lead:, :] = body


def gate_kernel(a_ref, b_ref, c_ref, ra_ref, rb_ref, rc_ref, tap_ref, out_ref, ext_ref):
    tokens = a_ref.shape[1]
    owners, channels, _ = out_ref.shape
    for slot in range(2):
        fill_extended(ext_ref, slot, (a_ref, b_ref, c_ref), (ra_ref, rb_ref, rc_ref), slot + 1)
    for start in range(0, tokens, LANES):
        key = short_filtered(tap_ref, 1, ext_ref, 0, tokens, start, LANES)
        value = short_filtered(tap_ref, 2, ext_ref, 1, tokens, start, LANES)
        turned_block = (key * value).T
        for p in range(owners):
            out_ref[p, :, start : start + LANES] = turned_block[p * channels : (p + 1) * channels]


def gate(parts, rims, taps, start, owners):
    count, tokens, width = parts[0].shape
    lead = rims[0].shape[1]
    channels = width // owners
    held = LANES // channels
    offset = start // LANES
    return pl.pallas_call(
        gate_kernel,
        grid=(width // LANES,),
        out_shape=jax.ShapeDtypeStruct((owners, channels, tokens), jnp.float32),
        in_specs=[pl.BlockSpec((count, tokens, LANES), lambda b: (0, 0, b))] * 3
        + [pl.BlockSpec((3, lead, LANES), lambda b: (0, 0, b + offset))] * 3
        + [pl.BlockSpec((3, 3, LANES), lambda b: (0, 0, b + offset))],
        out_specs=pl.BlockSpec((held, channels, tokens), lambda b: (b, 0, 0)),
        scratch_shapes=[pltpu.VMEM((2, lead + tokens, LANES), jnp.float32)],
        name="gate",
    )(*parts, *rims, taps)


def pack_kernel(chunks, owners, first_ref, filter_ref, skip_ref, out_ref):
    tokens = filter_ref.shape[0]
    for at in range(0, filter_ref.shape[1], LANES):
        start, width = next(c for c in chunks if c[0] <= at < c[0] + c[1])
        channels = width // owners
        for row in range(0, tokens, LANES):
            block = filter_ref[row : row + LANES, at : at + LANES]
            if row == 0:
                added = skip_ref[:, at : at + LANES] * first_ref[0].astype(jnp.float32)
                top = lax.broadcasted_iota(jnp.int32, block.shape, 0) == 0
                block = jnp.where(top, block + added, block)
            block = block.T
            for piece in range(LANES // channels):
                owner = (at - start) // channels + piece
                out_ref[
                    owner, start // owners : start // owners + channels, row : row + LANES
                ] = block[piece * channels : (piece + 1) * channels]


def pack_filter(long_filter, skip_gain, is_first, chunks, owners):
    tokens, width = long_filter.shape
    return pl.pallas_call(
        functools.partial(pack_kernel, chunks, owners),
        out_shape=jax.ShapeDtypeStruct((owners, width // owners, tokens), jnp.float32),
        in_specs=[pl.BlockSpec(memory_space=pltpu.SMEM), VMEM_SPEC, VMEM_SPEC],
        out_specs=VMEM_SPEC,
        name="pack_filter",
    )(is_first, long_filter, skip_gain)


def end_kernel(chunks, *refs):
    n = len(chunks)
    a_ref, b_ref, c_ref, ra_ref, rb_ref, rc_ref, tap_ref = refs[n : n + 7]
    out_ref, ext_ref = refs[n + 7 :]
    tokens, _ = out_ref.shape
    fill_extended(ext_ref, 0, (a_ref, b_ref, c_ref), (ra_ref, rb_ref, rc_ref), 0)
    for row in range(0, tokens, LANES):
        query = short_filtered(tap_ref, 0, ext_ref, 0, tokens, row, LANES)
        for ref, (start, width) in zip(refs[:n], chunks):
            owners, channels, _ = ref.shape
            block = ref[:, :, row : row + LANES].reshape(width, LANES)
            for at in range(0, width, LANES):
                cols = slice(start + at, start + at + LANES)
                out_ref[row : row + LANES, cols] = query[:, cols] * block[at : at + LANES].T


def end(convolved, chunks, parts, rims, taps):
    _, tokens, width = parts[0].shape
    lead = rims[0].shape[1]
    return pl.pallas_call(
        functools.partial(end_kernel, chunks),
        out_shape=jax.ShapeDtypeStruct((tokens, width), jnp.float32),
        in_specs=[VMEM_SPEC] * (len(chunks) + 7),
        out_specs=VMEM_SPEC,
        scratch_shapes=[pltpu.VMEM((1, lead + tokens, width), jnp.float32)],
        name="end",
    )(*convolved, *parts, *rims, taps)


def chunk_list(width, owners):
    grain = max(LANES, SUBLANES * owners)
    sizes = [2 * grain] if width >= 4 * grain else []
    while sum(sizes) < width:
        sizes.append(grain)
    starts = np.cumsum([0] + sizes[:-1]).tolist()
    return tuple(zip(starts, sizes))


def exchanged(block, axis, stride):
    size = lax.axis_size(axis)
    return lax.ppermute(block, axis, [(i, i ^ stride) for i in range(size)])


def on_device(sequence, w_proj, short_filter, long_filter, skip_gain):
    tokens = sequence.shape[0]
    width = long_filter.shape[1]
    owners = lax.axis_size("ctx")
    chunks = chunk_list(width, owners)
    weight = w_proj.transpose(1, 0, 2)
    col = lax.axis_index("col")
    owner = {d: (col ^ d)[None].astype(jnp.int32) for d in range(4)}
    forward, inverse, turns = tables(owners * tokens // LANES)
    turn_over = lambda block: lax.all_to_all(block, "ctx", 0, 0, tiled=True)

    def partial(rows, d, start, size, first, count):
        return project(rows, weight, owner[d], width, start, size, first, count)

    def summed(rows, start, size, first, count):
        to_far = exchanged(partial(rows, 3, start, size, first, count), "col", 1)
        far = partial(rows, 2, start, size, first, count) + to_far
        from_far = exchanged(far, "col", 2)
        near = exchanged(partial(rows, 1, start, size, first, count), "col", 1)
        return (partial(rows, 0, start, size, first, count), near, from_far)

    rim = sequence[tokens - SUBLANES :].astype(jnp.float32)
    shift = [(i, (i + 1) % owners) for i in range(owners)]
    rim = lax.ppermute(rim, "ctx", shift)

    parts = [summed(sequence, start, size, 1, 2) for start, size in chunks]
    is_first = (lax.axis_index("ctx") == 0)[None].astype(jnp.int32)
    packed = pack_filter(long_filter, skip_gain[None], is_first, chunks, owners)
    filter_spectrum = spectrum(turn_over(packed), forward, turns)
    rims = summed(rim, 0, width, 0, 3)
    query_parts = summed(sequence, 0, width, 0, 1)

    convolved = []
    for (start, size), chunk_parts in zip(chunks, parts):
        gated = turn_over(gate(chunk_parts, rims, short_filter, start, owners))
        done = convolve(gated, filter_spectrum, start // owners, forward, inverse, turns)
        convolved.append(turn_over(done))
    return end(convolved, chunks, query_parts, rims, short_filter)


def solution(mesh):
    return jax.shard_map(
        on_device,
        mesh=mesh,
        in_specs=(
            P("ctx", "col"),
            P("col", None, None),
            P(None, None, "col"),
            P("ctx", "col"),
            P("col"),
        ),
        out_specs=P("ctx", "col"),
        check_vma=False,
    )
```

```python
import functools
import math

import jax
import jax.numpy as jnp
import numpy as np
from jax import lax
from jax.experimental import pallas as pl
from jax.experimental.pallas import tpu as pltpu
from jax.sharding import PartitionSpec as P


LANES = 128
SUBLANES = 8

KERNEL_VMEM = 12 * 2**20
PROJECT_VMEM = 53 * 2**20
VMEM_SPEC = pl.BlockSpec(memory_space=pltpu.VMEM)


def turned(pair, count, length):
    real, imag = pair
    c = math.cos(2.0 * math.pi * count / length)
    s = math.sin(2.0 * math.pi * count / length)
    return (real * c + imag * s, imag * c - real * s)


def real_forward(blocks):
    count = len(blocks)
    if count == 2:
        return [(blocks[0] + blocks[1], None), (blocks[0] - blocks[1], None)]
    half, quarter = count // 2, count // 4
    even, odd = real_forward(blocks[0::2]), real_forward(blocks[1::2])
    terms = [None] * (half + 1)
    for k in range(quarter + 1):
        even_real, even_imag = even[k]
        if k == 0:
            terms[0] = (even_real + odd[0][0], None)
            terms[half] = (even_real - odd[0][0], None)
        elif k == quarter:
            terms[k] = (even_real, -odd[k][0])
        else:
            odd_real, odd_imag = turned(odd[k], k, count)
            terms[k] = (even_real + odd_real, even_imag + odd_imag)
            terms[half - k] = (even_real - odd_real, odd_imag - even_imag)
    return terms


def real_inverse(terms):
    half = len(terms) - 1
    count = 2 * half
    if count == 2:
        return [terms[0][0] + terms[1][0], terms[0][0] - terms[1][0]]
    quarter = half // 2
    even, odd = [], []
    for k in range(quarter + 1):
        (a_real, a_imag), (b_real, b_imag) = terms[k], terms[half - k]
        if k == 0:
            even.append((a_real + b_real, None))
            odd.append((a_real - b_real, None))
        elif k == quarter:
            even.append((2.0 * a_real, None))
            odd.append((-2.0 * a_imag, None))
        else:
            even.append((a_real + b_real, a_imag - b_imag))
            odd.append(turned((a_real - b_real, a_imag + b_imag), -k, count))
    result = [None] * count
    result[0::2] = real_inverse(even)
    result[1::2] = real_inverse(odd)
    return result


def split_table(table):
    table = jnp.asarray(table, jnp.float32)
    high = table.astype(jnp.bfloat16)
    return jnp.stack([high, (table - high.astype(jnp.float32)).astype(jnp.bfloat16)])


def tables(blocks):
    step = np.arange(LANES)
    angle = 2.0 * np.pi / LANES * (step[:, None] * step[None, :] % LANES)
    c, s = np.cos(angle), np.sin(angle)
    forward = np.block([[c, -s], [s, c]])
    total = blocks * LANES
    turn = 2.0 * np.pi / total * (np.arange(blocks // 2 + 1)[:, None] * step[None, :])
    turns = np.stack([np.cos(turn), np.sin(turn)])[:, :, None, :]
    return (
        split_table(forward),
        split_table(forward.T),
        jnp.asarray(turns, jnp.float32),
    )


def split_dot(left, table_ref):
    high = left.astype(jnp.bfloat16)
    low = (left - high.astype(jnp.float32)).astype(jnp.bfloat16)
    dot = functools.partial(jnp.dot, preferred_element_type=jnp.float32)
    return dot(high, table_ref[0]) + (dot(low, table_ref[0]) + dot(high, table_ref[1]))


def lane_blocks(ref, rows):
    sources, _, width = ref.shape
    return [
        ref[p, rows, i * LANES : (i + 1) * LANES]
        for p in range(sources)
        for i in range(width // LANES)
    ]


def forward_rows(in_ref, stage_ref, turns_ref):
    channels = in_ref.shape[1]

    def group(g, carry):
        rows = pl.ds(pl.multiple_of(g * SUBLANES, SUBLANES), SUBLANES)
        for k, (real, imag) in enumerate(real_forward(lane_blocks(in_ref, rows))):
            c, s = turns_ref[0, k], turns_ref[1, k]
            if imag is None:
                stage_ref[k, rows, :LANES] = real * c
                stage_ref[k, rows, LANES:] = -(real * s)
            else:
                stage_ref[k, rows, :LANES] = real * c + imag * s
                stage_ref[k, rows, LANES:] = imag * c - real * s
        return carry

    lax.fori_loop(0, channels // SUBLANES, group, 0)


def convolve_kernel(
    in_ref, spectrum_ref, forward_ref, inverse_ref, turns_ref, out_ref, stage_ref
):
    terms, channels, width = stage_ref.shape
    forward_rows(in_ref, stage_ref, turns_ref)
    rows = stage_ref[...].reshape(terms * channels, width)
    signal = split_dot(rows, forward_ref)
    other = spectrum_ref[...].reshape(terms * channels, width)
    s_real, s_imag = signal[:, :LANES], signal[:, LANES:]
    f_real, f_imag = other[:, :LANES], other[:, LANES:]
    product = jnp.concatenate(
        [s_real * f_real - s_imag * f_imag, s_real * f_imag + s_imag * f_real], axis=1
    )
    stage_ref[...] = split_dot(product, inverse_ref).reshape(terms, channels, width)
    _, _, tokens = in_ref.shape
    per_source = tokens // LANES

    def group(g, carry):
        group_rows = pl.ds(pl.multiple_of(g * SUBLANES, SUBLANES), SUBLANES)
        pairs = []
        for k in range(terms):
            real = stage_ref[k, group_rows, :LANES]
            imag = stage_ref[k, group_rows, LANES:]
            c, s = turns_ref[0, k], turns_ref[1, k]
            pairs.append((real * c - imag * s, imag * c + real * s))
        for m, block in enumerate(real_inverse(pairs)):
            i = m % per_source
            out_ref[m // per_source, group_rows, i * LANES : (i + 1) * LANES] = block
        return carry

    lax.fori_loop(0, channels // SUBLANES, group, 0)


def stage_shape(shape):
    sources, channels, tokens = shape
    return (sources * tokens // LANES // 2 + 1, channels, 2 * LANES)


def call(kernel, out_shape, operands, scratch=(), after=(), scalar=None, hbm=(), vmem=KERNEL_VMEM):
    wrapped = kernel
    n_scalar, n_in = int(scalar is not None), len(operands) + len(hbm)
    if after:

        def wrapped(*refs):
            return kernel(*refs[: n_scalar + n_in], *refs[n_scalar + n_in + len(after) :])

    anywhere = pl.BlockSpec(memory_space=pl.ANY)
    stays = pl.BlockSpec(memory_space=pltpu.HBM)
    specs = [VMEM_SPEC] * len(operands) + [stays] * len(hbm) + [anywhere] * len(after)
    lead = ()
    if scalar is not None:
        specs, lead = [pl.BlockSpec(memory_space=pltpu.SMEM)] + specs, (scalar,)
    return pl.pallas_call(
        wrapped,
        out_shape=out_shape,
        in_specs=specs,
        out_specs=jax.tree.map(lambda _: VMEM_SPEC, out_shape),
        scratch_shapes=list(scratch),
        compiler_params=pltpu.CompilerParams(vmem_limit_bytes=vmem),
    )(*lead, *operands, *hbm, *after)


def f32(*shape):
    return jax.ShapeDtypeStruct(shape, jnp.float32)


def spectrum_kernel(scale, offsets, in_ref, table_ref, turns_ref, *refs):
    out_refs, stage_ref = refs[:-1], refs[-1]
    terms, _, width = stage_ref.shape
    forward_rows(in_ref, stage_ref, turns_ref)
    for out_ref, first in zip(out_refs, offsets):
        count = out_ref.shape[1]
        rows = stage_ref[:, first : first + count, :].reshape(terms * count, width)
        out_ref[...] = (split_dot(rows, table_ref) * scale).reshape(terms, count, width)


def spectrum(received, forward, turns, chunks, after):
    owners, channels, tokens = received.shape
    terms, _, width = stage_shape(received.shape)
    return call(
        functools.partial(
            spectrum_kernel, 1.0 / (owners * tokens), [start // owners for start, _ in chunks]
        ),
        [f32(terms, size // owners, width) for _, size in chunks],
        (received, forward, turns),
        scratch=[pltpu.VMEM((terms, channels, width), jnp.float32)],
        after=after,
    )


def convolve_apart_kernel(me_ref, *refs):
    ins, outs, (stage_ref, whole_ref) = refs[:5], refs[5:-2], refs[-2:]
    convolve_kernel(*ins, whole_ref, stage_ref)
    for k, out_ref in enumerate(outs):
        out_ref[...] = whole_ref[me_ref[0] ^ k]


def convolve(received, filter_spectrum, forward, inverse, turns, me=None, after=()):
    operands = (received, filter_spectrum, forward, inverse, turns)
    stage = pltpu.VMEM(stage_shape(received.shape), jnp.float32)
    if me is None:
        return call(convolve_kernel, f32(*received.shape), operands, (stage,), after)
    return call(
        convolve_apart_kernel,
        [f32(*received.shape[1:])] * received.shape[0],
        operands,
        (stage, pltpu.VMEM(received.shape, jnp.float32)),
        after,
        me,
    )


def project_kernel(tasks, owner_width, load_rows, owner_ref, *refs):
    if load_rows:
        x_hbm, w_ref = refs[:2]
        outs, (x_ref, held_ref, sems) = refs[2:-3], refs[-3:]
        rows_copy = pltpu.make_async_copy(x_hbm, x_ref, sems.at[len(tasks)])
        rows_copy.start()
    else:
        x_ref, w_ref = refs[:2]
        outs, (held_ref, sems) = refs[2:-2], refs[-2:]

    def copy(index):
        _, _, which, _, j, start, size = tasks[index]
        at = pl.multiple_of(owner_ref[which] * owner_width + start, LANES)
        return pltpu.make_async_copy(
            w_ref.at[j, :, pl.ds(at, size)],
            held_ref.at[index, :, pl.ds(0, size)],
            sems.at[index],
        )

    for index in range(len(tasks)):
        copy(index).start()
    if load_rows:
        rows_copy.wait()
    for index, (output, slot, _, rows, _, _, size) in enumerate(tasks):
        copy(index).wait()
        outs[output][slot] = jnp.dot(
            x_ref[0:rows], held_ref[index, :, 0:size], preferred_element_type=jnp.float32
        )


def project(rows, weight, owners, owner_width, pieces, after=(), load_rows=False):
    depth = weight.shape[1]
    tasks = tuple(
        (output, slot, which, count, j, start, size)
        for output, (which, count, js, start, size) in enumerate(pieces)
        for slot, j in enumerate(js)
    )
    widest = max(size for *_, size in pieces)
    scratch = [
        pltpu.VMEM((len(tasks), depth, widest), weight.dtype),
        pltpu.SemaphoreType.DMA((len(tasks) + 1,)),
    ]
    if load_rows:
        scratch = [pltpu.VMEM(rows.shape, rows.dtype)] + scratch
    return call(
        functools.partial(project_kernel, tasks, owner_width, load_rows),
        [f32(len(js), count, size) for _, count, js, _, size in pieces],
        () if load_rows else (rows,),
        scratch=scratch,
        after=after,
        scalar=owners,
        hbm=(rows, weight) if load_rows else (weight,),
        vmem=PROJECT_VMEM,
    )


def last_rows_kernel(x_ref, out_ref):
    out_ref[...] = x_ref[...].astype(jnp.float32)


def extend_kernel(rim_ref, x_ref, out_ref):
    lead = rim_ref.shape[0]
    out_ref[0:lead] = rim_ref[...].astype(out_ref.dtype)
    out_ref[lead:] = x_ref[...]


def short_filtered(tap_ref, j, ext_ref, slot, start, size):
    taken = lambda back: ext_ref[slot, pl.ds(SUBLANES + start - back, size), :]
    return (
        tap_ref[0, j : j + 1, :] * taken(0)
        + tap_ref[1, j : j + 1, :] * taken(1)
        + tap_ref[2, j : j + 1, :] * taken(2)
    )


def fill_extended(ext_ref, slot, cols, refs):
    near, core, far = refs[0], refs[1], refs[2:]
    if len(far) == 1:
        ext_ref[slot] = near[slot, :, cols] + core[slot, :, cols] + far[0][slot, :, cols]
        return
    for rows, ref in ((slice(0, SUBLANES), far[0]), (slice(SUBLANES, None), far[1])):
        ext_ref[slot, rows, :] = (
            near[slot, rows, cols] + core[slot, rows, cols] + ref[slot, :, cols]
        )


def gate_kernel(offset, *refs):
    parts, (tap_ref, out_ref, ext_ref) = refs[:-3], refs[-3:]
    width = parts[0].shape[2]
    _, channels, tokens = out_ref.shape
    for at in range(0, width, LANES):
        cols = slice(at, at + LANES)
        taps = tap_ref.at[:, :, offset + at : offset + at + LANES]
        for slot in range(2):
            fill_extended(ext_ref, slot, cols, parts)
        for start in range(0, tokens, LANES):
            key = short_filtered(taps, 1, ext_ref, 0, start, LANES)
            value = short_filtered(taps, 2, ext_ref, 1, start, LANES)
            block = (key * value).T
            for piece in range(LANES // channels):
                out_ref[at // channels + piece, :, start : start + LANES] = block[
                    piece * channels : (piece + 1) * channels
                ]


def gate(parts, taps, start, owners, after=()):
    _, rows, width = parts[0].shape
    return call(
        functools.partial(gate_kernel, start),
        f32(owners, width // owners, rows - SUBLANES),
        (*parts, taps),
        scratch=[pltpu.VMEM((2, rows, LANES), jnp.float32)],
        after=after,
    )


def pack_kernel(chunks, first_ref, filter_ref, skip_ref, out_ref):
    tokens = filter_ref.shape[0]
    owners = out_ref.shape[0]
    for at in range(0, filter_ref.shape[1], LANES):
        start, width = next(c for c in chunks if c[0] <= at < c[0] + c[1])
        channels = width // owners
        for row in range(0, tokens, LANES):
            block = filter_ref[row : row + LANES, at : at + LANES]
            if row == 0:
                added = skip_ref[:, at : at + LANES] * first_ref[0].astype(jnp.float32)
                top = lax.broadcasted_iota(jnp.int32, block.shape, 0) == 0
                block = jnp.where(top, block + added, block)
            block = block.T
            for piece in range(LANES // channels):
                owner = (at - start) // channels + piece
                out_ref[
                    owner, start // owners : start // owners + channels, row : row + LANES
                ] = block[piece * channels : (piece + 1) * channels]


def end_kernel(chunks, apart, me_ref, *refs):
    n = len(chunks)
    owners = refs[0].shape[0] if not apart else apart
    count = n - 1 + owners if apart else n
    parts, (tap_ref, out_ref, ext_ref, whole_ref) = refs[count:-4], refs[-4:]
    tokens, _ = out_ref.shape
    blocks = list(refs[:n])
    if apart:
        for k in range(owners):
            whole_ref[me_ref[0] ^ k] = refs[k][...]
        blocks = [whole_ref] + list(refs[owners:count])
    for ref, (start, width) in zip(blocks, chunks):
        channels = ref.shape[1]
        for at in range(start, start + width, LANES):
            cols = slice(at, at + LANES)
            fill_extended(ext_ref, 0, cols, parts)
            taps = tap_ref.at[:, :, cols]
            held = LANES // channels
            first = (at - start) // channels
            for row in range(0, tokens, LANES):
                query = short_filtered(taps, 0, ext_ref, 0, row, LANES)
                block = ref[first : first + held, :, row : row + LANES].reshape(LANES, LANES)
                out_ref[row : row + LANES, cols] = query * block.T


def chunk_list(width, owners):
    grain = max(LANES, SUBLANES * owners)
    size = max(grain, width // 2)
    return tuple((start, size) for start in range(0, width, size))


def exchanged(block, axis, stride):
    size = lax.axis_size(axis)
    return lax.ppermute(block, axis, [(i, i ^ stride) for i in range(size)])


def on_device(sequence, w_proj, short_filter, long_filter, skip_gain):
    tokens, depth = sequence.shape
    width = long_filter.shape[1]
    owners = lax.axis_size("ctx")
    chunks = chunk_list(width, owners)
    weight = w_proj.transpose(1, 0, 2)
    col = lax.axis_index("col")
    owner = jnp.stack([col ^ d for d in range(4)]).astype(jnp.int32)
    forward, inverse, turns = tables(owners * tokens // LANES)
    rows = tokens + SUBLANES
    both = (1, 2)

    def turn_over(block):
        return lax.all_to_all(block, "ctx", 0, 0, tiled=True)

    def swap(block, stride):
        return exchanged(block, "col", stride)

    start, size = chunks[0]
    sent, kept = project(
        sequence,
        weight,
        owner,
        width,
        [(3, tokens, both, start, size), (2, tokens, both, start, size)],
        load_rows=True,
    )
    first_far = kept + swap(sent, 1)
    first_body = swap(first_far, 2)

    rim = call(
        last_rows_kernel, f32(SUBLANES, depth), (sequence[tokens - SUBLANES :],), after=(first_far,)
    )
    rim_got = lax.ppermute(rim, "ctx", [(i, (i + 1) % owners) for i in range(owners)])
    packed = call(
        functools.partial(pack_kernel, chunks),
        f32(owners, width // owners, tokens),
        (long_filter, skip_gain[None]),
        after=(rim,),
        scalar=(lax.axis_index("ctx") == 0)[None].astype(jnp.int32),
    )
    filter_got = turn_over(packed)
    extended = call(
        extend_kernel,
        jax.ShapeDtypeStruct((rows, depth), sequence.dtype),
        (rim_got, sequence),
        after=(packed,),
    )

    def pieces(far, near):
        listed = [(far, SUBLANES, both, start, size)]
        listed += [(far, rows, both, start, size) for start, size in chunks[1:]]
        return listed + [(far, rows, (0,), 0, width), (near, rows, both, start, size)]

    sent = project(extended, weight, owner, width, pieces(3, 1))
    kept = project(extended, weight, owner, width, pieces(2, 0), after=sent[:1])
    got = [swap(s, 1) for s in sent]
    far_sums = [k + g for k, g in zip(kept[:-1], got)]
    far = [swap(s, 2) for s in far_sums]
    far_parts = [(far[0], first_body)] + [(f,) for f in far[1:]]
    parts = [(kept[-1], got[-1])]

    def gated_chunk(index, after):
        part = (*parts[index], *far_parts[index])
        return gate(part, short_filter, chunks[index][0], owners, after)

    gated = gated_chunk(0, tuple(far_sums))

    def pieces(near):
        listed = [(near, rows, both, start, size) for start, size in chunks[1:]]
        return listed + [(near, rows, (0,), 0, width)]

    sent = project(extended, weight, owner, width, pieces(1), after=(gated,))
    kept = project(extended, weight, owner, width, pieces(0), after=sent[:1])
    parts += [(k, swap(s, 1)) for k, s in zip(kept, sent)]
    spectra = spectrum(filter_got, forward, turns, chunks, tuple(kept[:1]))
    last = len(chunks) - 1
    me = lax.axis_index("ctx")[None].astype(jnp.int32)
    convolved, done = [], spectra[0]
    for index in range(len(chunks)):
        arrived = turn_over(gated)
        apart = index == 0 < last
        done = convolve(
            arrived, spectra[index], forward, inverse, turns, me if apart else None
        )
        if index < last:
            gated = gated_chunk(index + 1, tuple(done[:1]) if apart else (done,))
        if apart:
            convolved.append(done[0])
            for k in range(1, owners):
                convolved.append(exchanged(done[k], "ctx", k))
        else:
            convolved.append(turn_over(done))
    return call(
        functools.partial(end_kernel, chunks, owners if last else 0),
        f32(tokens, width),
        (*convolved, *parts[-1], *far_parts[-1], short_filter),
        scratch=[
            pltpu.VMEM((1, rows, LANES), jnp.float32),
            pltpu.VMEM((owners, chunks[0][1] // owners, tokens), jnp.float32),
        ],
        scalar=me,
    )


def solution(mesh):
    return jax.shard_map(
        on_device,
        mesh=mesh,
        in_specs=(
            P("ctx", "col"),
            P("col", None, None),
            P(None, None, "col"),
            P("ctx", "col"),
            P("col"),
        ),
        out_specs=P("ctx", "col"),
        check_vma=False,
    )
```

```python
import functools
import math

import jax
import jax.numpy as jnp
import numpy as np
from jax import lax
from jax.experimental import pallas as pl
from jax.experimental.pallas import tpu as pltpu
from jax.sharding import PartitionSpec as P


LANES = 128
SUBLANES = 8

KERNEL_VMEM = 16 * 2**20
VMEM_SPEC = pl.BlockSpec(memory_space=pltpu.VMEM)


def turned(pair, count, length):
    real, imag = pair
    c = math.cos(2.0 * math.pi * count / length)
    s = math.sin(2.0 * math.pi * count / length)
    return (real * c + imag * s, imag * c - real * s)


def real_forward(blocks):
    count = len(blocks)
    if count == 2:
        return [(blocks[0] + blocks[1], None), (blocks[0] - blocks[1], None)]
    half, quarter = count // 2, count // 4
    even, odd = real_forward(blocks[0::2]), real_forward(blocks[1::2])
    terms = [None] * (half + 1)
    for k in range(quarter + 1):
        even_real, even_imag = even[k]
        if k == 0:
            terms[0] = (even_real + odd[0][0], None)
            terms[half] = (even_real - odd[0][0], None)
        elif k == quarter:
            terms[k] = (even_real, -odd[k][0])
        else:
            odd_real, odd_imag = turned(odd[k], k, count)
            terms[k] = (even_real + odd_real, even_imag + odd_imag)
            terms[half - k] = (even_real - odd_real, odd_imag - even_imag)
    return terms


def real_inverse(terms):
    half = len(terms) - 1
    count = 2 * half
    if count == 2:
        return [terms[0][0] + terms[1][0], terms[0][0] - terms[1][0]]
    quarter = half // 2
    even, odd = [], []
    for k in range(quarter + 1):
        (a_real, a_imag), (b_real, b_imag) = terms[k], terms[half - k]
        if k == 0:
            even.append((a_real + b_real, None))
            odd.append((a_real - b_real, None))
        elif k == quarter:
            even.append((2.0 * a_real, None))
            odd.append((-2.0 * a_imag, None))
        else:
            even.append((a_real + b_real, a_imag - b_imag))
            odd.append(turned((a_real - b_real, a_imag + b_imag), -k, count))
    result = [None] * count
    result[0::2] = real_inverse(even)
    result[1::2] = real_inverse(odd)
    return result


def split_table(table):
    table = jnp.asarray(table, jnp.float32)
    high = table.astype(jnp.bfloat16)
    return jnp.stack([high, (table - high.astype(jnp.float32)).astype(jnp.bfloat16)])


def tables(blocks):
    step = np.arange(LANES)
    angle = 2.0 * np.pi / LANES * (step[:, None] * step[None, :] % LANES)
    c, s = np.cos(angle), np.sin(angle)
    forward = np.block([[c, -s], [s, c]])
    total = blocks * LANES
    turn = 2.0 * np.pi / total * (np.arange(blocks // 2 + 1)[:, None] * step[None, :])
    turns = np.stack([np.cos(turn), np.sin(turn)])[:, :, None, :]
    return (
        split_table(forward),
        split_table(forward.T),
        jnp.asarray(turns, jnp.float32),
    )


def split_dot(left, table_ref):
    high = left.astype(jnp.bfloat16)
    low = (left - high.astype(jnp.float32)).astype(jnp.bfloat16)
    dot = functools.partial(jnp.dot, preferred_element_type=jnp.float32)
    return dot(high, table_ref[0]) + (dot(low, table_ref[0]) + dot(high, table_ref[1]))


def lane_blocks(ref, rows):
    sources, _, width = ref.shape
    return [
        ref[p, rows, i * LANES : (i + 1) * LANES]
        for p in range(sources)
        for i in range(width // LANES)
    ]


def forward_rows(in_ref, stage_ref, turns_ref):
    channels = stage_ref.shape[1]

    def group(g, carry):
        rows = pl.ds(pl.multiple_of(g * SUBLANES, SUBLANES), SUBLANES)
        for k, (real, imag) in enumerate(real_forward(lane_blocks(in_ref, rows))):
            c, s = turns_ref[0, k], turns_ref[1, k]
            if imag is None:
                stage_ref[k, rows, :LANES] = real * c
                stage_ref[k, rows, LANES:] = -(real * s)
            else:
                stage_ref[k, rows, :LANES] = real * c + imag * s
                stage_ref[k, rows, LANES:] = imag * c - real * s
        return carry

    lax.fori_loop(0, channels // SUBLANES, group, 0)


def convolve_kernel(count, *refs):
    scalars, refs = (refs[:1], refs[1:]) if count > 1 else ((), refs)
    in_ref, turns_ref, *sources = refs[:5]
    outs, (whole_ref, stage_ref, *held, sems) = refs[5 : 5 + count], refs[5 + count :]
    copies = [
        pltpu.make_async_copy(source, target, sems.at[i])
        for i, (source, target) in enumerate(zip(sources, held))
    ]
    for copy in copies:
        copy.start()
    forward_ref, spectrum_ref, inverse_ref = held
    terms, channels, width = stage_ref.shape
    forward_rows(in_ref, stage_ref, turns_ref)
    rows = stage_ref[...].reshape(terms * channels, width)
    copies[0].wait()
    signal = split_dot(rows, forward_ref)
    copies[1].wait()
    other = spectrum_ref[...].reshape(terms * channels, width)
    s_real, s_imag = signal[:, :LANES], signal[:, LANES:]
    f_real, f_imag = other[:, :LANES], other[:, LANES:]
    product = jnp.concatenate(
        [s_real * f_real - s_imag * f_imag, s_real * f_imag + s_imag * f_real], axis=1
    )
    copies[2].wait()
    stage_ref[...] = split_dot(product, inverse_ref).reshape(terms, channels, width)
    per_source = in_ref.shape[2] // LANES

    def group(g, carry):
        group_rows = pl.ds(pl.multiple_of(g * SUBLANES, SUBLANES), SUBLANES)
        pairs = []
        for k in range(terms):
            real = stage_ref[k, group_rows, :LANES]
            imag = stage_ref[k, group_rows, LANES:]
            c, s = turns_ref[0, k], turns_ref[1, k]
            pairs.append((real * c - imag * s, imag * c + real * s))
        for m, block in enumerate(real_inverse(pairs)):
            lanes = slice(m % per_source * LANES, (m % per_source + 1) * LANES)
            whole_ref[m // per_source, group_rows, lanes] = block
        return carry

    lax.fori_loop(0, channels // SUBLANES, group, 0)
    if count == 1:
        outs[0][...] = whole_ref[...]
    else:
        for k, out_ref in enumerate(outs):
            out_ref[...] = whole_ref[scalars[0][0] ^ k]


def stage_shape(shape):
    sources, channels, tokens = shape
    return (sources * tokens // LANES // 2 + 1, channels, 2 * LANES)


def call(kernel, out_shape, operands, scratch=(), after=(), scalar=None, hbm=()):
    wrapped = kernel
    n_scalar, n_in = int(scalar is not None), len(operands) + len(hbm)
    if after:

        def wrapped(*refs):
            return kernel(*refs[: n_scalar + n_in], *refs[n_scalar + n_in + len(after) :])

    anywhere = pl.BlockSpec(memory_space=pl.ANY)
    stays = pl.BlockSpec(memory_space=pltpu.HBM)
    hbm = [pltpu.with_memory_space_constraint(array, pltpu.HBM) for array in hbm]
    specs = [VMEM_SPEC] * len(operands) + [stays] * len(hbm) + [anywhere] * len(after)
    lead = ()
    if scalar is not None:
        specs, lead = [pl.BlockSpec(memory_space=pltpu.SMEM)] + specs, (scalar,)
    return pl.pallas_call(
        wrapped,
        out_shape=out_shape,
        in_specs=specs,
        out_specs=jax.tree.map(lambda _: VMEM_SPEC, out_shape),
        scratch_shapes=list(scratch),
        compiler_params=pltpu.CompilerParams(vmem_limit_bytes=KERNEL_VMEM),
    )(*lead, *operands, *hbm, *after)


def f32(*shape):
    return jax.ShapeDtypeStruct(shape, jnp.float32)


def spectrum_kernel(scale, first, in_ref, table_ref, turns_ref, out_ref):
    terms, channels, width = out_ref.shape
    forward_rows(in_ref.at[:, first : first + channels, :], out_ref, turns_ref)
    rows = out_ref[...].reshape(terms * channels, width)
    out_ref[...] = (split_dot(rows, table_ref) * scale).reshape(terms, channels, width)


def spectrum(received, first, channels, forward, turns, after):
    owners, _, tokens = received.shape
    return call(
        functools.partial(spectrum_kernel, 1.0 / (owners * tokens), first),
        f32(*stage_shape((owners, channels, tokens))),
        (received, forward, turns),
        after=after,
    )


def convolve(received, taps, forward, inverse, turns, me=None, after=()):
    vmem = lambda array: pltpu.VMEM(array.shape, array.dtype)
    count = 1 if me is None else received.shape[0]
    shapes = [f32(*received.shape)] if me is None else [f32(*received.shape[1:])] * count
    return call(
        functools.partial(convolve_kernel, count),
        shapes,
        (received, turns),
        (
            vmem(received),
            pltpu.VMEM(stage_shape(received.shape), jnp.float32),
            vmem(forward),
            vmem(taps),
            vmem(inverse),
            pltpu.SemaphoreType.DMA((3,)),
        ),
        after,
        me,
        (forward, taps, inverse),
    )


def project_kernel(tasks, owner_width, load_rows, owner_ref, *refs):
    if load_rows:
        x_hbm, w_ref = refs[:2]
        outs, (x_ref, held_ref, sems) = refs[2:-3], refs[-3:]
        rows_copy = pltpu.make_async_copy(x_hbm, x_ref, sems.at[len(tasks)])
        rows_copy.start()
    else:
        x_ref, w_ref = refs[:2]
        outs, (held_ref, sems) = refs[2:-2], refs[-2:]

    def copy(index):
        _, _, which, _, j, start, size = tasks[index]
        at = pl.multiple_of(owner_ref[which] * owner_width + start, LANES)
        return pltpu.make_async_copy(
            w_ref.at[j, :, pl.ds(at, size)],
            held_ref.at[index, :, pl.ds(0, size)],
            sems.at[index],
        )

    for index in range(len(tasks)):
        copy(index).start()
    if load_rows:
        rows_copy.wait()
    for index, (output, slot, _, rows, _, _, size) in enumerate(tasks):
        copy(index).wait()
        outs[output][slot] = jnp.dot(
            x_ref[0:rows], held_ref[index, :, 0:size], preferred_element_type=jnp.float32
        )


def project(rows, weight, owners, owner_width, pieces, after=(), load_rows=False):
    depth = weight.shape[1]
    tasks = tuple(
        (output, slot, which, count, j, start, size)
        for output, (which, count, js, start, size) in enumerate(pieces)
        for slot, j in enumerate(js)
    )
    widest = max(size for *_, size in pieces)
    scratch = [
        pltpu.VMEM((len(tasks), depth, widest), weight.dtype),
        pltpu.SemaphoreType.DMA((len(tasks) + 1,)),
    ]
    if load_rows:
        scratch = [pltpu.VMEM(rows.shape, rows.dtype)] + scratch
    return call(
        functools.partial(project_kernel, tasks, owner_width, load_rows),
        [f32(len(js), count, size) for _, count, js, _, size in pieces],
        () if load_rows else (rows,),
        scratch=scratch,
        after=after,
        scalar=owners,
        hbm=(rows, weight) if load_rows else (weight,),
    )


def last_rows_kernel(x_ref, out_ref):
    out_ref[...] = x_ref[...].astype(jnp.float32)


def extend_kernel(rim_ref, x_ref, out_ref):
    lead = rim_ref.shape[0]
    out_ref[0:lead] = rim_ref[...].astype(out_ref.dtype)
    out_ref[lead:] = x_ref[...]


def short_filtered(tap_ref, j, ext_ref, slot, start, size):
    taken = lambda back: ext_ref[slot, pl.ds(SUBLANES + start - back, size), :]
    return (
        tap_ref[0, j : j + 1, :] * taken(0)
        + tap_ref[1, j : j + 1, :] * taken(1)
        + tap_ref[2, j : j + 1, :] * taken(2)
    )


def fill_extended(ext_ref, slot, cols, refs):
    near, core, far = refs[0], refs[1], refs[2:]
    if len(far) == 1:
        ext_ref[slot] = near[slot, :, cols] + core[slot, :, cols] + far[0][slot, :, cols]
        return
    for rows, ref in ((slice(0, SUBLANES), far[0]), (slice(SUBLANES, None), far[1])):
        ext_ref[slot, rows, :] = (
            near[slot, rows, cols] + core[slot, rows, cols] + ref[slot, :, cols]
        )


def gate_kernel(offset, *refs):
    parts, (taps_ref, out_ref, ext_ref) = refs[:-3], refs[-3:]
    width = parts[0].shape[2]
    _, channels, tokens = out_ref.shape
    for at in range(0, width, LANES):
        cols = slice(at, at + LANES)
        taps = taps_ref.at[:, :, offset + at : offset + at + LANES]
        for slot in range(2):
            fill_extended(ext_ref, slot, cols, parts)
        for start in range(0, tokens, LANES):
            key = short_filtered(taps, 1, ext_ref, 0, start, LANES)
            value = short_filtered(taps, 2, ext_ref, 1, start, LANES)
            block = (key * value).T
            for piece in range(LANES // channels):
                out_ref[at // channels + piece, :, start : start + LANES] = block[
                    piece * channels : (piece + 1) * channels
                ]


def gate(parts, taps, start, owners, after=()):
    _, rows, width = parts[0].shape
    return call(
        functools.partial(gate_kernel, start),
        f32(owners, width // owners, rows - SUBLANES),
        (*parts, taps),
        scratch=[pltpu.VMEM((2, rows, LANES), jnp.float32)],
        after=tuple(after),
    )


def pack_kernel(chunks, first_ref, filter_ref, skip_ref, out_ref):
    tokens = filter_ref.shape[0]
    owners = out_ref.shape[0]
    for at in range(0, filter_ref.shape[1], LANES):
        start, width = next(c for c in chunks if c[0] <= at < c[0] + c[1])
        channels = width // owners
        for row in range(0, tokens, LANES):
            block = filter_ref[row : row + LANES, at : at + LANES]
            if row == 0:
                added = skip_ref[:, at : at + LANES] * first_ref[0].astype(jnp.float32)
                top = lax.broadcasted_iota(jnp.int32, block.shape, 0) == 0
                block = jnp.where(top, block + added, block)
            block = block.T
            for piece in range(LANES // channels):
                owner = (at - start) // channels + piece
                out_ref[
                    owner, start // owners : start // owners + channels, row : row + LANES
                ] = block[piece * channels : (piece + 1) * channels]


def rows_of(ref, channel, row):
    channels = ref.shape[1]
    first, held = channel // channels, LANES // channels
    return ref[first : first + held, :, row : row + LANES].reshape(LANES, LANES).T


def query_kernel(width, owners, me_ref, *refs):
    blocks, parts = refs[:owners], refs[owners:-4]
    tap_ref, out_ref, ext_ref, whole_ref = refs[-4:]
    for k in range(owners):
        whole_ref[me_ref[0] ^ k] = blocks[k][...]
    for at in range(0, out_ref.shape[1], LANES):
        cols = slice(at, at + LANES)
        fill_extended(ext_ref, 0, cols, parts)
        taps = tap_ref.at[:, :, cols]
        for row in range(0, out_ref.shape[0], LANES):
            query = short_filtered(taps, 0, ext_ref, 0, row, LANES)
            if at < width:
                query = query * rows_of(whole_ref, at, row)
            out_ref[row : row + LANES, cols] = query


def end_kernel(first, query_ref, convolved_ref, out_ref):
    tokens, width = out_ref.shape
    out_ref[:, :first] = query_ref[:, :first]
    for row in range(0, tokens, LANES):
        rows = slice(row, row + LANES)
        for at in range(first, width, LANES):
            cols = slice(at, at + LANES)
            out_ref[rows, cols] = query_ref[rows, cols] * rows_of(convolved_ref, at - first, row)


def halves(width, owners):
    size = max(width // 2, max(LANES, SUBLANES * owners))
    return ((0, size), (size, width - size))


def exchanged(block, axis, stride):
    size = lax.axis_size(axis)
    return lax.ppermute(block, axis, [(i, i ^ stride) for i in range(size)])


def on_device(sequence, w_proj, short_filter, long_filter, skip_gain):
    tokens, depth = sequence.shape
    width = long_filter.shape[1]
    owners = lax.axis_size("ctx")
    chunks = halves(width, owners)
    weight = w_proj.transpose(1, 0, 2)
    col = lax.axis_index("col")
    owner = jnp.stack([col ^ d for d in range(4)]).astype(jnp.int32)
    forward, inverse, turns = tables(owners * tokens // LANES)
    rows = tokens + SUBLANES
    both = (1, 2)

    def turn_over(block):
        return lax.all_to_all(block, "ctx", 0, 0, tiled=True)

    def swap(block, stride):
        return exchanged(block, "col", stride)

    start, size = chunks[0]
    sent, kept = project(
        sequence,
        weight,
        owner,
        width,
        [(3, tokens, both, start, size), (2, tokens, both, start, size)],
        load_rows=True,
    )
    sent_far = swap(sent, 1)

    packed = call(
        functools.partial(pack_kernel, chunks),
        f32(owners, width // owners, tokens),
        (long_filter, skip_gain[None]),
        after=(sent,),
        scalar=(lax.axis_index("ctx") == 0)[None].astype(jnp.int32),
    )
    rim = call(
        last_rows_kernel, f32(SUBLANES, depth), (sequence[tokens - SUBLANES :],), after=(sent,)
    )
    rim_got = lax.ppermute(rim, "ctx", [(i, (i + 1) % owners) for i in range(owners)])
    first_far = kept + sent_far
    first_body = swap(first_far, 2)
    filter_got = turn_over(packed)
    extended = call(
        extend_kernel,
        jax.ShapeDtypeStruct((rows, depth), sequence.dtype),
        (rim_got, sequence),
        after=(packed, first_far),
    )

    def both_ways(pieces, after=()):
        listed = [(3 - 2 * y, *piece) for y, *piece in pieces]
        listed += [(2 - 2 * y, *piece) for y, *piece in pieces]
        results = project(extended, weight, owner, width, listed, after)
        sent, kept = results[: len(pieces)], results[len(pieces) :]
        return [(k, swap(s, 1)) for k, s in zip(kept, sent)]

    first, second = chunks
    query = (rows, (0,), 0, width)
    far_rim, far_second = both_ways([(0, SUBLANES, both, *first), (0, rows, both, *second)])
    near_first, far_query = both_ways([(1, rows, both, *first), (0, *query)], (far_second[0],))
    got_rim = swap(far_rim[0] + far_rim[1], 2)
    sum_second = far_second[0] + far_second[1]
    got_second = swap(sum_second, 2)
    sum_query = far_query[0] + far_query[1]
    got_query = swap(sum_query, 2)

    channels = [size // owners for _, size in chunks]
    gated = gate(
        (*near_first, got_rim, first_body),
        short_filter,
        first[0],
        owners,
        after=(sum_second, sum_query),
    )
    arrived = turn_over(gated)
    near_second = both_ways([(1, rows, both, *second)], (gated,))[0]
    taps = [near_second[0]]
    for index in range(2):
        begin = index * channels[0]
        taps.append(
            spectrum(filter_got, begin, channels[index], forward, turns, (taps[-1],))
        )
    gated = gate((*near_second, got_second), short_filter, second[0], owners, after=taps[2:])
    me = lax.axis_index("ctx")[None].astype(jnp.int32)
    apart = convolve(arrived, taps[1], forward, inverse, turns, me, (gated,))
    arrived = turn_over(gated)
    back = [apart[0]]
    for k in range(1, owners):
        back.append(exchanged(apart[k], "ctx", k))
    done = convolve(arrived, taps[2], forward, inverse, turns)[0]
    convolved = turn_over(done)
    near_query = both_ways([(1, *query)], (done,))[0]
    queries = call(
        functools.partial(query_kernel, first[1], owners),
        f32(tokens, width),
        (*back, *near_query, got_query, short_filter),
        scratch=[
            pltpu.VMEM((1, rows, LANES), jnp.float32),
            pltpu.VMEM((owners, channels[0], tokens), jnp.float32),
        ],
        scalar=me,
        after=(done,),
    )
    return call(functools.partial(end_kernel, first[1]), f32(tokens, width), (queries, convolved))


def solution(mesh):
    return jax.shard_map(
        on_device,
        mesh=mesh,
        in_specs=(
            P("ctx", "col"),
            P("col", None, None),
            P(None, None, "col"),
            P("ctx", "col"),
            P("col"),
        ),
        out_specs=P("ctx", "col"),
        check_vma=False,
    )
```

```python
import functools
import math

import jax
import jax.numpy as jnp
import numpy as np
from jax import lax
from jax.experimental import pallas as pl
from jax.experimental.pallas import tpu as pltpu
from jax.sharding import PartitionSpec as P


LANES = 128
SUBLANES = 8

KERNEL_ROOM = 3 * 2**20
VMEM_SPEC = pl.BlockSpec(memory_space=pltpu.VMEM)


def turned(pair, count, length):
    real, imag = pair
    c = math.cos(2.0 * math.pi * count / length)
    s = math.sin(2.0 * math.pi * count / length)
    return (real * c + imag * s, imag * c - real * s)


def real_forward(blocks):
    count = len(blocks)
    if count == 2:
        return [(blocks[0] + blocks[1], None), (blocks[0] - blocks[1], None)]
    half, quarter = count // 2, count // 4
    even, odd = real_forward(blocks[0::2]), real_forward(blocks[1::2])
    terms = [None] * (half + 1)
    for k in range(quarter + 1):
        even_real, even_imag = even[k]
        if k == 0:
            terms[0] = (even_real + odd[0][0], None)
            terms[half] = (even_real - odd[0][0], None)
        elif k == quarter:
            terms[k] = (even_real, -odd[k][0])
        else:
            odd_real, odd_imag = turned(odd[k], k, count)
            terms[k] = (even_real + odd_real, even_imag + odd_imag)
            terms[half - k] = (even_real - odd_real, odd_imag - even_imag)
    return terms


def real_inverse(terms):
    half = len(terms) - 1
    count = 2 * half
    if count == 2:
        return [terms[0][0] + terms[1][0], terms[0][0] - terms[1][0]]
    quarter = half // 2
    even, odd = [], []
    for k in range(quarter + 1):
        (a_real, a_imag), (b_real, b_imag) = terms[k], terms[half - k]
        if k == 0:
            even.append((a_real + b_real, None))
            odd.append((a_real - b_real, None))
        elif k == quarter:
            even.append((2.0 * a_real, None))
            odd.append((-2.0 * a_imag, None))
        else:
            even.append((a_real + b_real, a_imag - b_imag))
            odd.append(turned((a_real - b_real, a_imag + b_imag), -k, count))
    result = [None] * count
    result[0::2] = real_inverse(even)
    result[1::2] = real_inverse(odd)
    return result


def split_table(table):
    table = jnp.asarray(table, jnp.float32)
    high = table.astype(jnp.bfloat16)
    return jnp.stack([high, (table - high.astype(jnp.float32)).astype(jnp.bfloat16)])


def tables(blocks):
    step = np.arange(LANES)
    angle = 2.0 * np.pi / LANES * (step[:, None] * step[None, :] % LANES)
    c, s = np.cos(angle), np.sin(angle)
    forward = np.block([[c, -s], [s, c]])
    total = blocks * LANES
    turn = 2.0 * np.pi / total * (np.arange(blocks // 2 + 1)[:, None] * step[None, :])
    turns = np.stack([np.cos(turn), np.sin(turn)])[:, :, None, :]
    return (
        split_table(forward),
        split_table(forward.T),
        jnp.asarray(turns, jnp.float32),
    )


def split_dot(left, table_ref):
    high = left.astype(jnp.bfloat16)
    low = (left - high.astype(jnp.float32)).astype(jnp.bfloat16)
    dot = functools.partial(jnp.dot, preferred_element_type=jnp.float32)
    return dot(high, table_ref[0]) + (dot(low, table_ref[0]) + dot(high, table_ref[1]))


def lane_blocks(ref, rows):
    sources, _, width = ref.shape
    return [
        ref[p, rows, i * LANES : (i + 1) * LANES]
        for p in range(sources)
        for i in range(width // LANES)
    ]


def forward_group(in_ref, stage_ref, turns_ref, g):
    rows = slice(g * SUBLANES, (g + 1) * SUBLANES)
    for k, (real, imag) in enumerate(real_forward(lane_blocks(in_ref, rows))):
        c, s = turns_ref[0, k], turns_ref[1, k]
        if imag is None:
            stage_ref[k, rows, :LANES] = real * c
            stage_ref[k, rows, LANES:] = -(real * s)
        else:
            stage_ref[k, rows, :LANES] = real * c + imag * s
            stage_ref[k, rows, LANES:] = imag * c - real * s


def spectrum_kernel(scale, first, in_ref, table_ref, turns_ref, out_ref):
    terms, channels, width = out_ref.shape
    for g in range(channels // SUBLANES):
        forward_group(in_ref.at[:, first : first + channels, :], out_ref, turns_ref, g)
    rows = out_ref[...].reshape(terms * channels, width)
    out_ref[...] = (split_dot(rows, table_ref) * scale).reshape(terms, channels, width)


def spectrum(received, first, channels, forward, turns, after):
    owners, _, tokens = received.shape
    return call(
        functools.partial(spectrum_kernel, 1.0 / (owners * tokens), first),
        f32(*stage_shape((owners, channels, tokens))),
        (received, forward, turns),
        after=after,
    )


def convolve_kernel(count, *refs):
    scalars, refs = (refs[:1], refs[1:]) if count > 1 else ((), refs)
    turns_ref, source_ref, *sources = refs[:5]
    outs, (*landing, whole_ref, stage_ref, a_ref, b_ref, c_ref, sems) = (
        refs[5 : 5 + count],
        refs[5 + count :],
    )
    held, in_ref = (a_ref, b_ref, c_ref), landing[0] if landing else source_ref
    terms, channels, width = stage_ref.shape
    groups = [slice(lo, lo + SUBLANES) for lo in range(0, channels, SUBLANES)]
    started = []

    def start(source, target):
        copy = pltpu.make_async_copy(source, target, sems.at[len(started)])
        copy.start()
        started.append(copy)
        return copy

    arriving = [
        start(source_ref.at[:, rows, :], in_ref.at[:, rows, :]) for rows in groups if landing
    ]
    forward_copy, spectrum_copy, inverse_copy = [start(s, t) for s, t in zip(sources, held)]
    forward_ref, spectrum_ref, inverse_ref = held
    for g in range(len(groups)):
        if landing:
            arriving[g].wait()
        forward_group(in_ref, stage_ref, turns_ref, g)
    rows = stage_ref[...].reshape(terms * channels, width)
    forward_copy.wait()
    signal = split_dot(rows, forward_ref)
    spectrum_copy.wait()
    other = spectrum_ref[...].reshape(terms * channels, width)
    s_real, s_imag = signal[:, :LANES], signal[:, LANES:]
    f_real, f_imag = other[:, :LANES], other[:, LANES:]
    product = jnp.concatenate(
        [s_real * f_real - s_imag * f_imag, s_real * f_imag + s_imag * f_real], axis=1
    )
    inverse_copy.wait()
    stage_ref[...] = split_dot(product, inverse_ref).reshape(terms, channels, width)
    per_source = in_ref.shape[2] // LANES
    leaving = []
    for group_rows in groups:
        pairs = []
        for k in range(terms):
            real = stage_ref[k, group_rows, :LANES]
            imag = stage_ref[k, group_rows, LANES:]
            c, s = turns_ref[0, k], turns_ref[1, k]
            pairs.append((real * c - imag * s, imag * c + real * s))
        for m, block in enumerate(real_inverse(pairs)):
            lanes = slice(m % per_source * LANES, (m % per_source + 1) * LANES)
            whole_ref[m // per_source, group_rows, lanes] = block
        if count == 1:
            leaving.append(start(whole_ref.at[:, group_rows, :], outs[0].at[:, group_rows, :]))
        else:
            leaving += [
                start(whole_ref.at[scalars[0][0] ^ k, group_rows, :], out_ref.at[group_rows, :])
                for k, out_ref in enumerate(outs)
            ]
    for copy in leaving:
        copy.wait()


def stage_shape(shape):
    sources, channels, tokens = shape
    return (sources * tokens // LANES // 2 + 1, channels, 2 * LANES)


def call(
    kernel,
    out_shape,
    operands,
    scratch=(),
    after=(),
    scalar=None,
    hbm=(),
    hbm_out=lambda index: False,
):
    wrapped = kernel
    n_scalar, n_in = int(scalar is not None), len(operands) + len(hbm)
    if after:

        def wrapped(*refs):
            return kernel(*refs[: n_scalar + n_in], *refs[n_scalar + n_in + len(after) :])

    anywhere = pl.BlockSpec(memory_space=pl.ANY)
    stays = pl.BlockSpec(memory_space=pltpu.HBM)
    hbm = [pltpu.with_memory_space_constraint(array, pltpu.HBM) for array in hbm]
    specs = [VMEM_SPEC] * len(operands) + [stays] * len(hbm) + [anywhere] * len(after)
    lead = ()
    if scalar is not None:
        specs, lead = [pl.BlockSpec(memory_space=pltpu.SMEM)] + specs, (scalar,)
    single = not isinstance(out_shape, list)
    shapes = [out_shape] if single else out_shape
    out_specs = [stays if hbm_out(index) else VMEM_SPEC for index in range(len(shapes))]
    results = pl.pallas_call(
        wrapped,
        out_shape=shapes,
        in_specs=specs,
        out_specs=out_specs,
        scratch_shapes=list(scratch),
        compiler_params=pltpu.CompilerParams(
            vmem_limit_bytes=vmem_needed(operands, shapes, scratch)
        ),
    )(*lead, *operands, *hbm, *after)
    return results[0] if single else results


def vmem_needed(operands, shapes, scratch):
    arrays = [*operands, *shapes, *(s for s in scratch if hasattr(s, "shape"))]
    total = 0
    for array in arrays:
        if jnp.issubdtype(array.dtype, jnp.number):
            *outer, rows, lanes = array.shape
            padded = math.prod(outer) * -(-rows // SUBLANES) * SUBLANES
            total += padded * -(-lanes // LANES) * LANES * jnp.dtype(array.dtype).itemsize
    return total + total // 8 + KERNEL_ROOM


def f32(*shape):
    return jax.ShapeDtypeStruct(shape, jnp.float32)


def convolve(received, taps, forward, inverse, turns, me=None, after=()):
    vmem = lambda array: pltpu.VMEM(array.shape, array.dtype)
    owners, channels, _ = received.shape
    count = 1 if me is None else owners
    shapes = [f32(*received.shape)] if me is None else [f32(*received.shape[1:])] * count
    return call(
        functools.partial(convolve_kernel, count),
        shapes,
        (turns,) if me is not None else (turns, received),
        (
            *([] if me is None else [vmem(received)]),
            vmem(received),
            pltpu.VMEM(stage_shape(received.shape), jnp.float32),
            vmem(forward),
            vmem(taps),
            vmem(inverse),
            pltpu.SemaphoreType.DMA((3 + channels // SUBLANES * (1 + count),)),
        ),
        after,
        me,
        (*([] if me is None else [received]), forward, taps, inverse),
        hbm_out=lambda index: True,
    )


def project_kernel(tasks, owner_width, load_rows, owner_ref, *refs):
    if load_rows:
        x_hbm, w_ref = refs[:2]
        outs, (x_ref, held_ref, sems) = refs[2:-3], refs[-3:]
        rows_copy = pltpu.make_async_copy(x_hbm, x_ref, sems.at[len(tasks)])
        rows_copy.start()
    else:
        x_ref, w_ref = refs[:2]
        outs, (held_ref, sems) = refs[2:-2], refs[-2:]

    def copy(index):
        _, _, which, _, j, start, size = tasks[index]
        at = pl.multiple_of(owner_ref[which] * owner_width + start, LANES)
        return pltpu.make_async_copy(
            w_ref.at[j, :, pl.ds(at, size)],
            held_ref.at[index, :, pl.ds(0, size)],
            sems.at[index],
        )

    for index in range(len(tasks)):
        copy(index).start()
    if load_rows:
        rows_copy.wait()
    for index, (output, slot, _, rows, _, _, size) in enumerate(tasks):
        copy(index).wait()
        outs[output][slot] = jnp.dot(
            x_ref[0:rows], held_ref[index, :, 0:size], preferred_element_type=jnp.float32
        )


def project(rows, weight, owners, owner_width, pieces, after=(), load_rows=False):
    depth = weight.shape[1]
    tasks = tuple(
        (output, slot, which, count, j, start, size)
        for output, (which, count, js, start, size) in enumerate(pieces)
        for slot, j in enumerate(js)
    )
    widest = max(size for *_, size in pieces)
    scratch = [
        pltpu.VMEM((len(tasks), depth, widest), weight.dtype),
        pltpu.SemaphoreType.DMA((len(tasks) + 1,)),
    ]
    if load_rows:
        scratch = [pltpu.VMEM(rows.shape, rows.dtype)] + scratch
    return call(
        functools.partial(project_kernel, tasks, owner_width, load_rows),
        [f32(len(js), count, size) for _, count, js, _, size in pieces],
        () if load_rows else (rows,),
        scratch=scratch,
        after=after,
        scalar=owners,
        hbm=(rows, weight) if load_rows else (weight,),
    )


def last_rows_kernel(x_ref, out_ref):
    out_ref[...] = x_ref[...].astype(jnp.float32)


def extend_kernel(rim_ref, x_ref, out_ref):
    lead = rim_ref.shape[0]
    out_ref[0:lead] = rim_ref[...].astype(out_ref.dtype)
    out_ref[lead:] = x_ref[...]


def short_filtered(tap_ref, j, ext_ref, slot, start, size):
    taken = lambda back: ext_ref[slot, pl.ds(SUBLANES + start - back, size), :]
    return (
        tap_ref[0, j : j + 1, :] * taken(0)
        + tap_ref[1, j : j + 1, :] * taken(1)
        + tap_ref[2, j : j + 1, :] * taken(2)
    )


def fill_extended(ext_ref, slot, cols, near, far):
    total = near[0][slot, :, cols]
    for ref in near[1:]:
        total = total + ref[slot, :, cols]
    if len(far) == 1:
        ext_ref[slot] = total + far[0][slot, :, cols]
    else:
        ext_ref[slot, :SUBLANES, :] = total[:SUBLANES] + far[0][slot, :, cols]
        ext_ref[slot, SUBLANES:, :] = total[SUBLANES:] + far[1][slot, :, cols]


def gate_kernel(near_count, far_count, *refs):
    near, far = refs[:near_count], refs[near_count : near_count + far_count]
    taps_ref, out_ref, ext_ref = *refs[near_count + far_count : -2][:1], *refs[-2:]
    held, channels, tokens = out_ref.shape
    for slot in range(2):
        fill_extended(ext_ref, slot, slice(0, LANES), near, far)
    for start in range(0, tokens, LANES):
        key = short_filtered(taps_ref, 1, ext_ref, 0, start, LANES)
        value = short_filtered(taps_ref, 2, ext_ref, 1, start, LANES)
        block = (key * value).T
        for piece in range(held):
            out_ref[piece, :, start : start + LANES] = block[
                piece * channels : (piece + 1) * channels
            ]


def gate(near, far, taps, start, owners, after=()):
    _, rows, width = near[0].shape
    channels, offset = width // owners, start // LANES
    part = lambda array: pl.BlockSpec((*array.shape[:2], LANES), lambda b: (0, 0, b))
    out_block = (LANES // channels, channels, rows - SUBLANES)
    out_shape = f32(owners, channels, rows - SUBLANES)
    scratch = [pltpu.VMEM((2, rows, LANES), jnp.float32)]
    needed = vmem_needed((*near, *far), [out_shape], scratch)
    return pl.pallas_call(
        functools.partial(gate_kernel, len(near), len(far)),
        grid=(width // LANES,),
        out_shape=out_shape,
        in_specs=[part(array) for array in (*near, *far)]
        + [pl.BlockSpec((3, 3, LANES), lambda b: (0, 0, b + offset))]
        + [pl.BlockSpec(memory_space=pl.ANY)] * len(after),
        out_specs=pl.BlockSpec(out_block, lambda b: (b, 0, 0)),
        scratch_shapes=scratch,
        compiler_params=pltpu.CompilerParams(vmem_limit_bytes=needed),
        name="gate",
    )(*near, *far, taps, *after)


def pack_kernel(chunks, first_ref, filter_ref, skip_ref, out_ref):
    tokens = filter_ref.shape[0]
    owners = out_ref.shape[0]
    for at in range(0, filter_ref.shape[1], LANES):
        start, width = next(c for c in chunks if c[0] <= at < c[0] + c[1])
        channels = width // owners
        for row in range(0, tokens, LANES):
            block = filter_ref[row : row + LANES, at : at + LANES]
            if row == 0:
                added = skip_ref[:, at : at + LANES] * first_ref[0].astype(jnp.float32)
                top = lax.broadcasted_iota(jnp.int32, block.shape, 0) == 0
                block = jnp.where(top, block + added, block)
            block = block.T
            for piece in range(LANES // channels):
                owner = (at - start) // channels + piece
                out_ref[
                    owner, start // owners : start // owners + channels, row : row + LANES
                ] = block[piece * channels : (piece + 1) * channels]


def rows_of(ref, channel, row):
    channels = ref.shape[1]
    first, held = channel // channels, LANES // channels
    return ref[first : first + held, :, row : row + LANES].reshape(LANES, LANES).T


def query_kernel(width, owners, me_ref, *refs):
    blocks, parts = refs[:owners], refs[owners:-4]
    tap_ref, out_ref, ext_ref, whole_ref = refs[-4:]
    for k in range(owners):
        whole_ref[me_ref[0] ^ k] = blocks[k][...]
    for at in range(0, out_ref.shape[1], LANES):
        cols = slice(at, at + LANES)
        fill_extended(ext_ref, 0, cols, parts[:2], parts[2:])
        taps = tap_ref.at[:, :, cols]
        for row in range(0, out_ref.shape[0], LANES):
            query = short_filtered(taps, 0, ext_ref, 0, row, LANES)
            if at < width:
                query = query * rows_of(whole_ref, at, row)
            out_ref[row : row + LANES, cols] = query


def end_kernel(first, query_ref, convolved_ref, out_ref):
    tokens, width = out_ref.shape
    out_ref[:, :first] = query_ref[:, :first]
    for row in range(0, tokens, LANES):
        rows = slice(row, row + LANES)
        for at in range(first, width, LANES):
            cols = slice(at, at + LANES)
            out_ref[rows, cols] = query_ref[rows, cols] * rows_of(convolved_ref, at - first, row)


def halves(width, owners):
    size = max(width // 2, max(LANES, SUBLANES * owners))
    return ((0, size), (size, width - size))


def exchanged(block, axis, stride):
    size = lax.axis_size(axis)
    return lax.ppermute(block, axis, [(i, i ^ stride) for i in range(size)])


def on_device(sequence, w_proj, short_filter, long_filter, skip_gain):
    tokens, depth = sequence.shape
    width = long_filter.shape[1]
    owners = lax.axis_size("ctx")
    chunks = halves(width, owners)
    weight = w_proj.transpose(1, 0, 2)
    col = lax.axis_index("col")
    owner = jnp.stack([col ^ d for d in range(4)]).astype(jnp.int32)
    forward, inverse, turns = tables(owners * tokens // LANES)
    rows = tokens + SUBLANES
    both = (1, 2)

    def turn_over(block):
        return lax.all_to_all(block, "ctx", 0, 0, tiled=True)

    def swap(block, stride):
        return exchanged(block, "col", stride)

    start, size = chunks[0]
    sent, kept = project(
        sequence,
        weight,
        owner,
        width,
        [(3, tokens, both, start, size), (2, tokens, both, start, size)],
        load_rows=True,
    )
    sent_far = swap(sent, 1)

    packed = call(
        functools.partial(pack_kernel, chunks),
        f32(owners, width // owners, tokens),
        (long_filter, skip_gain[None]),
        scalar=(lax.axis_index("ctx") == 0)[None].astype(jnp.int32),
    )
    rim = call(
        last_rows_kernel, f32(SUBLANES, depth), (sequence[tokens - SUBLANES :],), after=(sent,)
    )
    rim_got = lax.ppermute(rim, "ctx", [(i, (i + 1) % owners) for i in range(owners)])
    first_far = kept + sent_far
    first_body = swap(first_far, 2)
    filter_got = turn_over(packed)
    extended = call(
        extend_kernel,
        jax.ShapeDtypeStruct((rows, depth), sequence.dtype),
        (rim_got, sequence),
        after=(packed, first_far),
    )

    def both_ways(pieces, after=()):
        listed = [(3 - 2 * y, *piece) for y, *piece in pieces]
        listed += [(2 - 2 * y, *piece) for y, *piece in pieces]
        results = project(extended, weight, owner, width, listed, after)
        sent, kept = results[: len(pieces)], results[len(pieces) :]
        return [(k, swap(s, 1)) for k, s in zip(kept, sent)]

    first, second = chunks
    query = (rows, (0,), 0, width)
    far_rim, far_second = both_ways([(0, SUBLANES, both, *first), (0, rows, both, *second)])
    near_first, far_query = both_ways([(1, rows, both, *first), (0, *query)], (far_second[0],))
    got_rim = swap(far_rim[0] + far_rim[1], 2)
    sum_second = far_second[0] + far_second[1]
    got_second = swap(sum_second, 2)
    sum_query = far_query[0] + far_query[1]
    got_query = swap(sum_query, 2)

    channels = [size // owners for _, size in chunks]
    gated = gate(
        near_first,
        (got_rim, first_body),
        short_filter,
        first[0],
        owners,
        after=(sum_second, sum_query),
    )
    arrived = turn_over(gated)
    near_second = both_ways([(1, rows, both, *second)], (gated,))[0]
    taps = [near_second[0]]
    for index in range(2):
        begin = index * channels[0]
        taps.append(
            spectrum(filter_got, begin, channels[index], forward, turns, (taps[-1],))
        )
    near_sum = near_second[0] + near_second[1]
    gated = gate((near_sum,), (got_second,), short_filter, second[0], owners, tuple(taps[2:]))
    me = lax.axis_index("ctx")[None].astype(jnp.int32)
    apart = convolve(arrived, taps[1], forward, inverse, turns, me, (gated,))
    arrived = turn_over(gated)
    back = [apart[0]]
    for k in range(1, owners):
        back.append(exchanged(apart[k], "ctx", k))
    done = convolve(arrived, taps[2], forward, inverse, turns)[0]
    convolved = turn_over(done)
    near_query = both_ways([(1, *query)], (done,))[0]
    queries = call(
        functools.partial(query_kernel, first[1], owners),
        f32(tokens, width),
        (*back, *near_query, got_query, short_filter),
        scratch=[
            pltpu.VMEM((1, rows, LANES), jnp.float32),
            pltpu.VMEM((owners, channels[0], tokens), jnp.float32),
        ],
        scalar=me,
        after=(done,),
    )
    return call(functools.partial(end_kernel, first[1]), f32(tokens, width), (queries, convolved))


def solution(mesh):
    return jax.shard_map(
        on_device,
        mesh=mesh,
        in_specs=(
            P("ctx", "col"),
            P("col", None, None),
            P(None, None, "col"),
            P("ctx", "col"),
            P("col"),
        ),
        out_specs=P("ctx", "col"),
        check_vma=False,
    )
```
